256 devices in a mesh: corpus: 32 (over x, y, core), fsdp: 8 (over z).
Axes of the slice: x: 4, y: 4, z: 8, core: 2. Of those that a mesh axis runs over, the one named last changes fastest.
Arguments:
- queries: bfloat16 [1024, 2048], P(('corpus', 'fsdp')), may hold values from -16 to 16
- candidates: int32 [1024, 8], P(('corpus', 'fsdp')), may hold values from 0 to 1023, as said below
- tables: bfloat16 [1024, 20, 2048], P('corpus'), may hold values from -6 to 6
- lengths: int32 [1024], P('corpus'), may hold values from 5 to 20
- passage_embed: bfloat16 [1024, 2048], P('corpus'), may hold values from -6 to 6
- reader_weight: bfloat16 [2048, 2560], P(('corpus', 'fsdp')), may hold values from -0.125 to 0.125
- readout: float32 [2560], replicated, may hold values from -0.125 to 0.125
Outputs:
- query_grad: float32 [1024, 2048], P(('corpus', 'fsdp'))
- losses: float32 [1024], P(('corpus', 'fsdp'))
The draws below stay inside these ranges and needn't reach their ends.
Inputs may be any that keep to these rules, and one draw needn't show every extreme that they name: Tables 32 * j to 32 * j + 31 are held by index j of corpus. Among the 32 candidates of one device's queries at most 2 are held by any one index of corpus, and one index of corpus holds exactly 2 of every device's candidates.
All inputs are finite; a program needn't handle non-finite values.
Results may differ from the reference program's by a relative error of at most 0.0021.
Values may be sent and summed in bfloat16 or wider, within the bound.
A program may use at most 128 MiB of HBM per device.

```python
import math
import jax
import jax.numpy as jnp
from jax import lax

D = 2048
FF = 2560
CAND = 8
PLEN = 20
Q_DEV = 4
TAB_DEV = 32
NTAB = 1024
QUERIES = 1024
CAP = 2
N_CORPUS = 32
N_FSDP = 8


def owner_draw(key):
    blocks = N_CORPUS * N_FSDP
    per_block = Q_DEV * CAND
    slot_count = N_CORPUS * CAP
    slot_owner = jnp.arange(slot_count, dtype=jnp.int32) // CAP
    hot_owner = jax.random.randint(jax.random.fold_in(key, 3), (), 0, N_CORPUS)
    owner_weight = jax.random.randint(jax.random.fold_in(key, 4), (N_CORPUS,), 1, 5)
    base_score = jax.random.randint(jax.random.fold_in(key, 5), (blocks, slot_count), 0, 65536)
    ranking = base_score * owner_weight[slot_owner][None, :] + jnp.where(slot_owner == hot_owner, 524288, 0)[None, :]
    ranking = ranking * slot_count + jnp.arange(slot_count, dtype=jnp.int32)[None, :]
    top_values, chosen = lax.top_k(ranking, per_block)
    shuffle_score = jax.random.randint(jax.random.fold_in(key, 6), (blocks, per_block), 0, 65536) * per_block + jnp.arange(per_block, dtype=jnp.int32)[None, :]
    reorder = jnp.argsort(shuffle_score, axis=1)
    chosen = jnp.take_along_axis(chosen, reorder, axis=1)
    local_ids = jax.random.randint(jax.random.fold_in(key, 8), (blocks, per_block), 0, TAB_DEV)
    table_ids = chosen // CAP * TAB_DEV + local_ids
    return table_ids.astype(jnp.int32).reshape(QUERIES, CAND)


def embed_draw(key):
    return jnp.clip(jax.random.normal(jax.random.fold_in(key, 7), (NTAB, D), jnp.float32), -6.0, 6.0)


def draw_candidates(key, part):
    return owner_draw(key)


def draw_passage_embed(key, part):
    return embed_draw(key).astype(jnp.bfloat16)


def draw_queries(key, part):
    jitter = jnp.clip(jax.random.normal(jax.random.fold_in(key, 9), (QUERIES, D), jnp.float32), -6.0, 6.0)
    return jitter.astype(jnp.bfloat16)


def draw_lengths(key, part):
    drawn = jax.random.randint(jax.random.fold_in(key, 12), (NTAB,), max(1, PLEN // 4), PLEN + 1)
    longest = jax.random.randint(jax.random.fold_in(key, 13), (), 0, NTAB)
    return jnp.where(jnp.arange(NTAB) == longest, PLEN, drawn).astype(jnp.int32)


def steps_of(rng, dims, split, low, top_value):
    gain = 1.0
    for axis_at, shards_of in split:
        heights = jax.random.uniform(jax.random.fold_in(jax.random.fold_in(rng, 6), axis_at), (shards_of,), jnp.float32, low / len(split), top_value / len(split))
        gain = gain * jnp.repeat(jnp.exp(heights), dims[axis_at] // shards_of).reshape((-1,) + (1,) * (len(dims) - 1 - axis_at))
    return gain


def centred(rng, dims, deviation, limit, pieces=(), held_as=jnp.bfloat16):
    loudness = steps_of(rng, dims, pieces, -0.22, 0.18) if pieces else 1.0
    values = jax.random.normal(rng, dims, jnp.float32) * deviation * loudness
    return jnp.minimum(jnp.maximum(values, -limit), limit).astype(held_as)


def setup_inputs(seed: int = 0) -> dict:
    key_list = jax.random.split(jax.random.key(seed), 8)
    return {
        "queries": draw_queries(jax.random.fold_in(key_list[7], 71), 0),
        "candidates": draw_candidates(jax.random.fold_in(key_list[7], 71), 0),
        "tables": centred(key_list[2], (NTAB, PLEN, D), 1.0, 6.0, ((0, 32),)),
        "lengths": draw_lengths(jax.random.fold_in(key_list[7], 71), 0),
        "passage_embed": draw_passage_embed(jax.random.fold_in(key_list[7], 71), 0),
        "reader_weight": centred(key_list[5], (D, FF), D ** -0.5, 0.125, ((0, 256),)),
        "readout": centred(key_list[6], (FF,), FF ** -0.5, 0.125, (), jnp.float32),
    }


GELU_SCALE = math.sqrt(2.0 / math.pi)
GELU_CUBIC = 0.044715
LOSS_SCALE = 64.0

def gelu_pair(hidden):
    tanh_part = jnp.tanh(GELU_SCALE * (hidden + GELU_CUBIC * hidden * hidden * hidden))
    values = 0.5 * hidden * (1.0 + tanh_part)
    slopes = 0.5 * (1.0 + tanh_part) + 0.5 * hidden * (1.0 - tanh_part * tanh_part) * GELU_SCALE * (1.0 + 3.0 * GELU_CUBIC * hidden * hidden)
    return (values, slopes)

def read_tables(table_rows, table_lens, query_rows, weight, readout):
    count_rows, tok_len, width = table_rows.shape
    inputs = (table_rows.astype(jnp.float32) + query_rows.astype(jnp.float32)[:, None, :]).astype(jnp.bfloat16)
    hidden = jnp.dot(inputs.reshape(count_rows * tok_len, width), weight, preferred_element_type=jnp.float32)
    values, slopes = gelu_pair(hidden)
    readings = jnp.dot(values, readout, precision=lax.Precision.HIGHEST).reshape(count_rows, tok_len)
    positions = lax.broadcasted_iota(jnp.int32, (count_rows, tok_len), 1)
    valid_tok = (positions < table_lens[:, None]).astype(jnp.float32)
    weights_tok = valid_tok / table_lens[:, None].astype(jnp.float32)
    likeness = lax.optimization_barrier(jnp.sum(weights_tok * readings, axis=1))
    summed = jnp.einsum('mt,mtn->mn', weights_tok, slopes.reshape(count_rows, tok_len, -1), precision=lax.Precision.HIGHEST) * readout[None, :]
    towards = jnp.dot(summed.astype(jnp.bfloat16), weight.T, preferred_element_type=jnp.float32)
    return (likeness, towards)

def score_rows(query_rows, embeds):
    products = query_rows.astype(jnp.float32) * embeds.astype(jnp.float32)
    return lax.optimization_barrier(jnp.sum(products, axis=1)) / math.sqrt(embeds.shape[1])

def finish(scores, likeness, embeds, towards, query_count):
    width = embeds.shape[1]
    retrieve = scores.reshape(query_count, -1)
    joined = retrieve + likeness.reshape(query_count, -1)
    prior_prob = jax.nn.softmax(retrieve, axis=1)
    posterior = jax.nn.softmax(joined, axis=1)
    losses = jax.nn.logsumexp(retrieve, axis=1) - jax.nn.logsumexp(joined, axis=1)
    factors = (prior_prob - posterior) / math.sqrt(width)
    emb_three = embeds.astype(jnp.float32).reshape(query_count, -1, width)
    tow_three = towards.reshape(query_count, -1, width)
    first_part = jnp.einsum('qk,qkd->qd', factors, emb_three, precision=lax.Precision.HIGHEST)
    second_part = jnp.einsum('qk,qkd->qd', posterior, tow_three, precision=lax.Precision.HIGHEST)
    return (LOSS_SCALE * (first_part - second_part), losses)

def reference(queries, candidates, tables, lengths, passage_embed, reader_weight, readout):

    def one_block(paired):
        query_block, cand_block = paired
        flat_ids = cand_block.reshape(-1)
        query_rows = jnp.repeat(query_block, CAND, axis=0)
        embeds = passage_embed[flat_ids]
        likeness, towards = read_tables(tables[flat_ids], lengths[flat_ids], query_rows, reader_weight, readout)
        scores = score_rows(query_rows, embeds)
        return finish(scores, likeness, embeds, towards, Q_DEV)
    gradient, losses = lax.map(one_block, (queries.reshape(-1, Q_DEV, D), candidates.reshape(-1, Q_DEV, CAND)))
    return (gradient.reshape(QUERIES, D), losses.reshape(QUERIES))
```

```python
import functools
import math

import jax
import jax.numpy as jnp
from jax import lax
from jax.experimental import pallas as pl
from jax.experimental.pallas import tpu as pltpu
from jax.sharding import PartitionSpec as P

GELU_SCALE = math.sqrt(2.0 / math.pi)
GELU_CUBIC = 0.044715
LOSS_SCALE = 64.0
BETA = GELU_CUBIC / (GELU_SCALE * GELU_SCALE)
FAR = -1.0e5

MESH = pl.DeviceIdType.MESH
F32 = jnp.float32
BF16 = jnp.bfloat16
I32 = jnp.int32
NJ, NF = 32, 8
HID = 320
LANES = 384
SLOTS = NJ * 2


def iota(shape, dim):
    return lax.broadcasted_iota(I32, shape, dim)


def dot_nt(a, b):
    return lax.dot_general(a, b, (((1,), (1,)), ((), ())), preferred_element_type=F32)


def dot(a, b):
    return jnp.dot(a, b, preferred_element_type=F32)


def two(x):
    hi = x.astype(BF16)
    return hi, (x - hi.astype(F32)).astype(BF16)


def kernel(
    w_ref, q_ref, cand_ref, tab_ref, len_ref, emb_ref, ro_ref,
    grad_ref, loss_ref,
    wsl, ros, qz, wall, w2, x_s, tw0, tw, qw, linv, cidv, cid, emb32, lens_s, e32, esend, eall, acc, lvs, rsend, rall,
    zrow, zall, outp, orec,
    ws_sem, wr_sem, qs_sem, qr_sem, gs_sem, gr_sem, hs_sem, hr_sem, es_sem, er_sem, rs_sem, rr_sem,
    ls_sem, lr_sem, os_sem, or_sem, c_sem,
):
    j = lax.axis_index("corpus")
    f = lax.axis_index("fsdp")
    jx, jy, jc = j // 8, (j // 2) % 4, j % 2

    def remote(src, dst, ssem, rsem, jj, ff):
        return pltpu.make_async_remote_copy(
            src_ref=src, dst_ref=dst, send_sem=ssem, recv_sem=rsem, device_id=(jj, ff), device_id_type=MESH
        )

    load = pltpu.make_async_copy(tab_ref, x_s, c_sem.at[5])
    load.start()
    barrier = pltpu.get_barrier_semaphore()

    @pl.loop(1, NF)
    def _(i):
        pl.semaphore_signal(barrier, inc=1, device_id=(j, (f + i) % NF), device_id_type=MESH)

    @pl.loop(1, NJ)
    def _(i):
        pl.semaphore_signal(barrier, inc=1, device_id=((j + i) % NJ, f), device_id_type=MESH)

    cand = cand_ref[...].astype(F32)
    wide = jnp.concatenate([jnp.broadcast_to(cand[i : i + 1], (8, 8)) for i in range(4)], axis=0)
    eye = iota((32, 32), 0) == iota((32, 32), 1)
    idc = jnp.sum(jnp.where(iota((32, 8), 0) % 8 == iota((32, 8), 1), wide, 0.0), axis=1, keepdims=True)
    idr = jnp.sum(jnp.where(eye, idc, 0.0), axis=0, keepdims=True).astype(I32)
    idc = idc.astype(I32)
    own_r, own_c = idr // 32, idc // 32
    same = (own_c == own_r) & (iota((32, 32), 1) < iota((32, 32), 0))
    earlier = jnp.sum(jnp.where(same, 1, 0).astype(F32), axis=1, keepdims=True).astype(I32)
    lane_of = own_c * 2 + earlier + HID
    at_slot = lane_of == iota((32, LANES), 1)
    id_lane = jnp.sum(jnp.where(at_slot, (idc % 32 + 1).astype(F32), 0.0), axis=0, keepdims=True) - 1.0
    q_lane = jnp.sum(jnp.where(at_slot, (iota((32, LANES), 0) // 8).astype(F32), 0.0), axis=0, keepdims=True)
    row8, lane8 = iota((8, LANES), 0), iota((8, LANES), 1)
    tail = jnp.where(row8 == 0, id_lane, jnp.where(row8 == 1, q_lane, 0.0))
    w_own = w_ref[...].astype(F32)
    for g in range(NF):
        base, off = g * HID // 128 * 128, g * HID % 128
        seg, b = w_own[:, base : base + LANES], base // 128
        rseg = jnp.concatenate([jnp.broadcast_to(ro_ref[b + i : b + i + 1], (8, 128)) for i in range(3)], axis=1)
        if off:
            seg, rseg = pltpu.roll(seg, LANES - off, 1), pltpu.roll(rseg, LANES - off, 1)
        wsl[g] = jnp.where(lane8 < HID, seg, tail).astype(BF16)
        ros[g] = jnp.where(lane8 < HID, rseg, 0.0)
    len_col = jnp.sum(jnp.where(eye, len_ref[...].astype(F32), 0.0), axis=1, keepdims=True)
    lens_s[...] = jnp.broadcast_to(len_col, (32, 128))
    linv[...] = 1.0 / lens_s[...]
    emb32[...] = emb_ref[:, pl.ds(pl.multiple_of(f * 256, 256), 256)].astype(F32)

    pl.semaphore_wait(barrier, NF - 1 + NJ - 1)

    @pl.loop(1, NF)
    def _(i):
        g = (f + i) % NF
        remote(wsl.at[g], wall.at[j, f], ws_sem.at[g], wr_sem.at[f], j, g).start()

    @pl.loop(1, NF)
    def _(i):
        g = (f + i) % NF
        remote(q_ref, qz.at[f], qs_sem.at[g], qr_sem.at[f], j, g).start()

    own_w = pltpu.make_async_copy(wsl.at[f], wall.at[j, f], c_sem.at[0])
    own_q = pltpu.make_async_copy(q_ref, qz.at[f], c_sem.at[1])
    own_w.start()
    own_q.start()

    own_w.wait()

    @pl.loop(1, NF)
    def _(i):
        g = (f + i) % NF
        remote(wsl.at[g], wall.at[j, g], ws_sem.at[g], wr_sem.at[g], j, g).wait_recv()

    def at(x, y, c):
        return ((x + 4) % 4) * 8 + ((y + 4) % 4) * 2 + c

    def along(a, b):
        return at(jx + jnp.where(jc == 0, a, b), jy + jnp.where(jc == 0, b, a), jc)

    def gather(buf, ssem, rsem, width, between):
        sent = []

        def send(slot, part, to):
            if part is None:
                ref, sem = buf.at[slot], rsem.at[slot, 0]
            else:
                ref, sem = buf.at[slot, pl.ds(part * width, width)], rsem.at[slot, part]
            copy = remote(ref, ref, ssem.at[len(sent)], sem, to, f)
            copy.start()
            sent.append(copy)

        def wait(slot, part):
            if part is None:
                ref, sem = buf.at[slot], rsem.at[slot, 0]
            else:
                ref, sem = buf.at[slot, pl.ds(part * width, width)], rsem.at[slot, part]
            remote(ref, ref, ssem.at[0], sem, j ^ 1, f).wait_recv()

        up_a, dn_a, up_b, dn_b, mate = along(1, 0), along(-1, 0), along(0, 1), along(0, -1), at(jx, jy, 1 - jc)

        def first(slot):
            send(slot, None, up_b)
            send(slot, None, dn_b)
            send(slot, None, mate)

        send(j, None, up_a)
        send(j, None, dn_a)
        first(j)
        between()
        wait(dn_a, None)
        send(dn_a, 0, up_a)
        first(dn_a)
        wait(up_a, None)
        send(up_a, 1, dn_a)
        first(up_a)
        over = along(2, 0)

        def second(a):
            wait(along(a, -1), None)
            send(along(a, -1), 0, up_b)
            send(along(a, -1), None, mate)
            wait(along(a, 1), None)
            send(along(a, 1), 1, dn_b)
            send(along(a, 1), None, mate)

        second(0)
        wait(over, 0)
        wait(over, 1)
        first(over)
        second(-1)
        second(1)
        second(2)
        for a in (0, -1, 1, 2):
            wait(along(a, 2), 0)
            wait(along(a, 2), 1)
            send(along(a, 2), None, mate)

        @pl.loop(0, 16)
        def _(k):
            slot = k * 2 + 1 - jc
            remote(buf.at[slot], buf.at[slot], ssem.at[0], rsem.at[slot, 0], j ^ 1, f).wait_recv()

        return sent

    sent_w = gather(wall, gs_sem, gr_sem, 4, lambda: None)

    @pl.loop(0, NJ)
    def _(k):
        for h in range(4):
            pair = jnp.concatenate([wall[k, 2 * h].astype(F32), wall[k, 2 * h + 1].astype(F32)], axis=0)
            w2[pl.ds(pl.multiple_of(k * 64 + h * 16, 16), 16), :] = pair.astype(BF16)

    own_q.wait()

    @pl.loop(1, NF)
    def _(i):
        g = (f + i) % NF
        remote(q_ref, qz.at[g], qs_sem.at[g], qr_sem.at[g], j, g).wait_recv()

    q4 = [qz[g].astype(F32) for g in range(NF)]
    q32 = jnp.concatenate(q4, axis=0).astype(BF16)
    qw[j] = (dot(q32, w2[...]) * GELU_SCALE).reshape(2, 16, LANES)

    pick = (iota((8, 128), 1) == HID - 256 + 2 * j + iota((8, 128), 0)) & (iota((8, 128), 0) < 2)
    cidv[...] = dot_nt(jnp.where(pick, 1.0, 0.0).astype(BF16), w2[:, 256:LANES]).astype(I32)
    to_smem = pltpu.make_async_copy(cidv, cid, c_sem.at[2])
    to_smem.start()
    to_smem.wait()

    def during_queries():
        load.wait()

        @pl.loop(0, 4)
        def _(p):
            rows = pl.ds(pl.multiple_of(p * 160, 16), 160)
            part = dot(x_s[rows, :], w2[...]) * GELU_SCALE
            for b in range(3):
                tw0[b, rows, :] = part[:, b * 128 : (b + 1) * 128]

        @pl.loop(0, 8)
        def _(p):
            for i in range(4):
                c = p * 4 + i
                valid = iota((24, 128), 0).astype(F32) < lens_s[pl.ds(c, 1), :]
                for b in range(3):
                    part = tw0[b, pl.ds(c, 24, stride=32), :]
                    tw[c, :, b * 128 : (b + 1) * 128] = jnp.where(valid, part, FAR)

        @pl.loop(0, NJ)
        def _(i):
            k = (j + i) % NJ
            for s in range(16):
                c = jnp.clip(cid[s % 2, (k * 8 + s // 2) * 8], 0, 31)
                e32[pl.ds(s, 1), :] = emb32[pl.ds(c, 1), :]
            esend[k] = e32[...].astype(BF16)

    sent_q = gather(qw, hs_sem, hr_sem, 1, during_queries)

    @pl.loop(1, NJ)
    def _(i):
        k = (j + i) % NJ
        remote(esend.at[k], eall.at[j], es_sem.at[k], er_sem.at[j], k, f).start()

    own_e = pltpu.make_async_copy(esend.at[j], eall.at[j], c_sem.at[3])
    own_e.start()

    lane16 = iota((16, LANES), 1)
    ro16 = ros[f]
    ro_row = ro16[0:1]

    def send_block(k):
        remote(rsend.at[k], rall.at[j], rs_sem.at[k], rr_sem.at[j], k, f).start()

    @pl.loop(0, NJ)
    def _(i):
        k = (j + i) % NJ
        for s in range(16):
            d, e = s // 2, s % 2
            c = jnp.clip(cid[e, (k * 8 + d) * 8], 0, 31)
            q = jnp.clip(cid[e, (k * 8 + d) * 8 + 1], 0, 3)
            y = tw[c] + qw[k, d // 4, pl.ds((d % 4) * 4 + q, 1), :]
            y2 = y * y
            z = (y * BETA) * y2
            u = y + z
            t = jnp.tanh(u)
            c1 = 1.0 + t
            slope = c1 * ((1.0 - t) * (u + (z + z)) + 1.0)
            value = c1 * y
            slope = slope[0:8] + slope[8:16] + slope[16:24]
            value = (value[0:8] + value[8:16] + value[16:24]) * ro16
            value = value[:, 0:128] + value[:, 128:256] + value[:, 256:384]
            inv = linv[pl.ds(c, 1), :]
            lvs[pl.ds(s, 1), :] = jnp.sum(value, axis=0, keepdims=True) * inv
            slope = jnp.sum(slope, axis=0, keepdims=True)
            for b in range(3):
                acc[pl.ds(s, 1), b * 128 : (b + 1) * 128] = slope[:, b * 128 : (b + 1) * 128] * inv
        like = jnp.sum(lvs[...], axis=1, keepdims=True) * (0.5 / GELU_SCALE)
        summed = (acc[...] * 0.5) * ro_row
        hi = like.astype(BF16).astype(F32)
        mid = (like - hi).astype(BF16).astype(F32)
        low = like - hi - mid
        summed = jnp.where(lane16 == HID, hi, summed)
        summed = jnp.where(lane16 == HID + 1, mid, summed)
        summed = jnp.where(lane16 == HID + 2, low, summed)
        rsend[k] = summed.astype(BF16)

        @pl.when(i > 1)
        def _():
            send_block((j + i - 1) % NJ)

    send_block((j + NJ - 1) % NJ)
    own_r_copy = pltpu.make_async_copy(rsend.at[j], rall.at[j], c_sem.at[4])
    own_r_copy.start()

    own_e.wait()

    @pl.loop(1, NJ)
    def _(i):
        k = (j + i) % NJ
        remote(esend.at[k], eall.at[k], es_sem.at[k], er_sem.at[k], k, f).wait_recv()

    ev = eall[...].reshape(NJ * 16, 256)
    q64 = jnp.concatenate([qz[g, :, pl.ds(pl.multiple_of(f * 256, 256), 256)].astype(F32) for g in range(NF) for _ in range(2)], axis=0)
    sc = dot_nt(q64.astype(BF16), ev)

    r64, s64 = iota((64, 512), 0), iota((64, 512), 1)
    spread = jnp.where(iota((128, 512), 0) == HID - 256 + iota((128, 512), 1) // 16 * 2 + iota((128, 512), 1) % 2, 1.0, 0.0).astype(BF16)
    ids = [wall[j, g, :, 256:LANES].astype(F32) for g in range(NF)]
    id64 = jnp.concatenate([jnp.broadcast_to(v[0:1], (8, 128)) for v in ids], axis=0)
    qi64 = jnp.concatenate([jnp.broadcast_to(v[1:2], (8, 128)) for v in ids], axis=0)
    mine = (dot(id64.astype(BF16), spread) >= 0.0) & (dot(qi64.astype(BF16), spread).astype(I32) == r64 % 4)
    mine = mine & ((s64 // 2) % 8 == r64 // 8)
    score_row = jnp.sum(jnp.where(mine & ((r64 // 4) % 2 == 0), sc, 0.0), axis=0, keepdims=True)

    own_r_copy.wait()

    @pl.loop(1, NJ)
    def _(i):
        k = (j + i) % NJ
        remote(rsend.at[k], rall.at[k], rs_sem.at[k], rr_sem.at[k], k, f).wait_recv()

    rv = rall[...].reshape(NJ * 16, LANES)
    lp = (iota((8, LANES), 1) >= HID) & (iota((8, LANES), 1) < HID + 3)
    like_row = dot_nt(jnp.where(lp, 1.0, 0.0).astype(BF16), rv)[0:1]
    zrow[:, 0:512] = like_row
    zrow[:, 512:1024] = score_row

    @pl.loop(1, NF)
    def _(i):
        g = (f + i) % NF
        remote(zrow, zall.at[f], ls_sem.at[g], lr_sem.at[f], j, g).start()

    zall[f] = zrow[...]

    @pl.loop(1, NF)
    def _(i):
        g = (f + i) % NF
        remote(zrow, zall.at[g], ls_sem.at[g], lr_sem.at[g], j, g).wait_recv()

    total = zall[0]
    for g in range(1, NF):
        total = total + zall[g]
    retrieve = jnp.broadcast_to(total[:, 512:1024], (64, 512)) * (1.0 / math.sqrt(2048.0))
    joined = retrieve + jnp.broadcast_to(total[:, 0:512], (64, 512))

    def softmax(v):
        top = jnp.max(jnp.where(mine, v, -3.0e38), axis=1, keepdims=True)
        ex = jnp.where(mine, jnp.exp(jnp.where(mine, v - top, 0.0)), 0.0)
        norm = jnp.sum(ex, axis=1, keepdims=True)
        return ex / norm, top + jnp.log(norm)

    prior, lse_r = softmax(retrieve)
    post, lse_j = softmax(joined)
    loss = lse_r - lse_j
    own_row = (iota((64, 128), 0) == f * 8 + iota((64, 128), 1)) & (iota((64, 128), 1) < 4)
    loss_ref[...] = jnp.sum(jnp.where(own_row, loss, 0.0), axis=0, keepdims=True)[:, 0:4]

    hi, lo = two(post)
    mix = dot(hi, rv) + dot(lo, rv)
    mix = jnp.where(iota((64, LANES), 1) < HID, mix, 0.0)
    hi, lo = two(mix)
    fhi, flo = two((prior - post) * (LOSS_SCALE / math.sqrt(2048.0)))
    first = dot(fhi, ev) + dot(flo, ev)
    upper = (iota((64, 256), 0) // 4) % 2 == 1
    for b in range(4):
        w_lo, w_hi = w2[b * 256 : (b + 1) * 256, :], w2[1024 + b * 256 : 1024 + (b + 1) * 256, :]
        part = jnp.where(upper, dot_nt(hi, w_hi) + dot_nt(lo, w_hi), dot_nt(hi, w_lo) + dot_nt(lo, w_lo))
        place = ((f % 4) == b) & (upper == (f // 4 == 1))
        part = jnp.where(place, first, 0.0) - LOSS_SCALE * part
        outp[:, :, b * 256 : (b + 1) * 256] = part.reshape(NF, 8, 256)

    @pl.loop(1, NF)
    def _(i):
        g = (f + i) % NF
        remote(outp.at[g], orec.at[f], os_sem.at[g], or_sem.at[f], j, g).start()

    for copy in sent_w + sent_q:
        copy.wait_send()

    @pl.loop(1, NJ)
    def _(i):
        k = (j + i) % NJ
        remote(esend.at[k], eall.at[k], es_sem.at[k], er_sem.at[k], k, f).wait_send()
        remote(rsend.at[k], rall.at[k], rs_sem.at[k], rr_sem.at[k], k, f).wait_send()

    total8 = outp[f]

    @pl.loop(1, NF)
    def _(i):
        g = (f + i) % NF
        remote(wsl.at[g], wall.at[j, g], ws_sem.at[g], wr_sem.at[g], j, g).wait_send()
        remote(q_ref, qz.at[g], qs_sem.at[g], qr_sem.at[g], j, g).wait_send()
        remote(zrow, zall.at[g], ls_sem.at[g], lr_sem.at[g], j, g).wait_send()
        remote(outp.at[g], orec.at[g], os_sem.at[g], or_sem.at[g], j, g).wait()

    orec[f] = total8
    total8 = orec[0]
    for g in range(1, NF):
        total8 = total8 + orec[g]
    grad_ref[:, 0:1024] = total8[0:4]
    grad_ref[:, 1024:2048] = total8[4:8]


def on_device(queries, candidates, tables, lengths, passage_embed, reader_weight, readout):
    vm = pl.BlockSpec(memory_space=pltpu.VMEM)
    dma = pltpu.SemaphoreType.DMA
    grad, loss = pl.pallas_call(
        kernel,
        out_shape=(jax.ShapeDtypeStruct((4, 2048), F32), jax.ShapeDtypeStruct((1, 4), F32)),
        in_specs=[vm] * 3 + [pl.BlockSpec(memory_space=pl.ANY)] + [vm] * 3,
        out_specs=(vm, vm),
        scratch_shapes=[
            pltpu.VMEM((NF, 8, LANES), BF16),
            pltpu.VMEM((NF, 8, LANES), F32),
            pltpu.VMEM((NF, 4, 2048), BF16),
            pltpu.VMEM((NJ, NF, 8, LANES), BF16),
            pltpu.VMEM((2048, LANES), BF16),
            pltpu.VMEM((640, 2048), BF16),
            pltpu.VMEM((3, 768, 128), F32),
            pltpu.VMEM((32, 24, LANES), F32),
            pltpu.VMEM((NJ, 2, 16, LANES), F32),
            pltpu.VMEM((32, 128), F32),
            pltpu.VMEM((8, 2048), I32),
            pltpu.SMEM((8, 2048), I32),
            pltpu.VMEM((32, 256), F32),
            pltpu.VMEM((32, 128), F32),
            pltpu.VMEM((16, 256), F32),
            pltpu.VMEM((NJ, 16, 256), BF16),
            pltpu.VMEM((NJ, 16, 256), BF16),
            pltpu.VMEM((16, LANES), F32),
            pltpu.VMEM((16, 128), F32),
            pltpu.VMEM((NJ, 16, LANES), BF16),
            pltpu.VMEM((NJ, 16, LANES), BF16),
            pltpu.VMEM((1, 1024), F32),
            pltpu.VMEM((NF, 1, 1024), F32),
            pltpu.VMEM((NF, 8, 1024), F32),
            pltpu.VMEM((NF, 8, 1024), F32),
            dma((NF,)), dma((NF,)), dma((NF,)), dma((NF,)),
            dma((48,)), dma((NJ, 2)), dma((48,)), dma((NJ, 2)),
            dma((NJ,)), dma((NJ,)), dma((NJ,)), dma((NJ,)),
            dma((NF,)), dma((NF,)), dma((NF,)), dma((NF,)), dma((6,)),
        ],
        compiler_params=pltpu.CompilerParams(collective_id=0, has_side_effects=True, vmem_limit_bytes=50 << 20),
    )(
        reader_weight,
        queries,
        candidates,
        tables.transpose(1, 0, 2).reshape(640, 2048),
        lengths.reshape(1, 32),
        passage_embed,
        readout.reshape(20, 128),
    )
    return grad, loss.reshape(4)


def solution(mesh):
    both = ("corpus", "fsdp")
    in_specs = (P(both, None), P(both, None), P("corpus", None, None), P("corpus"), P("corpus", None), P(both, None), P())
    return jax.shard_map(
        on_device, mesh=mesh, in_specs=in_specs, out_specs=(P(both, None), P(both)), check_vma=False
    )
```

```python
import functools
import math

import jax
import jax.numpy as jnp
from jax import lax
from jax.experimental import pallas as pl
from jax.experimental.pallas import tpu as pltpu
from jax.sharding import PartitionSpec as P

GELU_SCALE = math.sqrt(2.0 / math.pi)
GELU_CUBIC = 0.044715
LOSS_SCALE = 64.0
BETA = GELU_CUBIC / (GELU_SCALE * GELU_SCALE)
FAR = -1.0e5

MESH = pl.DeviceIdType.MESH
F32 = jnp.float32
BF16 = jnp.bfloat16
I32 = jnp.int32
NJ, NF = 32, 8
HID = 320
LANES = 384
SLOTS = NJ * 2


def iota(shape, dim):
    return lax.broadcasted_iota(I32, shape, dim)


def dot_nt(a, b):
    return lax.dot_general(a, b, (((1,), (1,)), ((), ())), preferred_element_type=F32)


def dot(a, b):
    return jnp.dot(a, b, preferred_element_type=F32)


def two(x):
    hi = x.astype(BF16)
    return hi, (x - hi.astype(F32)).astype(BF16)


def kernel(
    w_hbm, q_hbm, cand_hbm, tab_hbm, len_hbm, emb_hbm, ro_hbm,
    grad_ref, loss_ref,
    w_ref, q_ref, cand_ref, len_ref, ro_ref, wsl, ros, qz, wall, w2, x_s, tw0, tw, tw3, qw, linv, cidv, cid, lens_s, emball, ev_s, mine_s, acc, lvs, rsend, rall,
    zrow, zall, srow, sall, outp, orec, tab, qcur,
    ws_sem, wr_sem, qs_sem, qr_sem, gs_sem, gr_sem, hs_sem, hr_sem, es_sem, er_sem, rs_sem, rr_sem,
    ls_sem, lr_sem, os_sem, or_sem, c_sem, i_sem, ss_sem, sr_sem,
):
    j = lax.axis_index("corpus")
    f = lax.axis_index("fsdp")
    jx, jy, jc = j // 8, (j // 2) % 4, j % 2

    def remote(src, dst, ssem, rsem, jj, ff):
        return pltpu.make_async_remote_copy(
            src_ref=src, dst_ref=dst, send_sem=ssem, recv_sem=rsem, device_id=(jj, ff), device_id_type=MESH
        )

    pairs = ((cand_hbm, cand_ref), (w_hbm, w_ref), (ro_hbm, ro_ref), (len_hbm, len_ref), (q_hbm, q_ref))
    pairs = pairs + ((emb_hbm.at[:, pl.ds(pl.multiple_of(f * 256, 256), 256)], emball.at[j]), (tab_hbm, x_s))
    loads = [pltpu.make_async_copy(a, b, i_sem.at[n]) for n, (a, b) in enumerate(pairs)]
    for load in loads:
        load.start()
    barrier = pltpu.get_barrier_semaphore()

    @pl.loop(1, NF)
    def _(i):
        pl.semaphore_signal(barrier, inc=1, device_id=(j, (f + i) % NF), device_id_type=MESH)

    @pl.loop(1, NJ)
    def _(i):
        pl.semaphore_signal(barrier, inc=1, device_id=((j + i) % NJ, f), device_id_type=MESH)

    for load in loads[:6]:
        load.wait()

    cand = cand_ref[...].astype(F32)
    wide = jnp.concatenate([jnp.broadcast_to(cand[i : i + 1], (8, 8)) for i in range(4)], axis=0)
    eye = iota((32, 32), 0) == iota((32, 32), 1)
    idc = jnp.sum(jnp.where(iota((32, 8), 0) % 8 == iota((32, 8), 1), wide, 0.0), axis=1, keepdims=True)
    idr = jnp.sum(jnp.where(eye, idc, 0.0), axis=0, keepdims=True).astype(I32)
    idc = idc.astype(I32)
    own_r, own_c = idr // 32, idc // 32
    same = (own_c == own_r) & (iota((32, 32), 1) < iota((32, 32), 0))
    earlier = jnp.sum(jnp.where(same, 1, 0).astype(F32), axis=1, keepdims=True).astype(I32)
    lane_of = own_c * 2 + earlier + HID
    at_slot = lane_of == iota((32, LANES), 1)
    id_lane = jnp.sum(jnp.where(at_slot, (idc % 32 + 1).astype(F32), 0.0), axis=0, keepdims=True) - 1.0
    q_lane = jnp.sum(jnp.where(at_slot, (iota((32, LANES), 0) // 8).astype(F32), 0.0), axis=0, keepdims=True)
    row8, lane8 = iota((8, LANES), 0), iota((8, LANES), 1)
    tail = jnp.where(row8 == 0, id_lane, jnp.where(row8 == 1, q_lane, 0.0))
    w_own = w_ref[...].astype(F32)
    for g in range(NF):
        base, off = g * HID // 128 * 128, g * HID % 128
        seg, b = w_own[:, base : base + LANES], base // 128
        rseg = jnp.concatenate([jnp.broadcast_to(ro_ref[b + i : b + i + 1], (8, 128)) for i in range(3)], axis=1)
        if off:
            seg, rseg = pltpu.roll(seg, LANES - off, 1), pltpu.roll(rseg, LANES - off, 1)
        wsl[g] = jnp.where(lane8 < HID, seg, tail).astype(BF16)
        ros[g] = jnp.where(lane8 < HID, rseg, pltpu.roll(rseg, 64, 1))
    len_col = jnp.sum(jnp.where(eye, len_ref[...].astype(F32), 0.0), axis=1, keepdims=True)
    lens_s[...] = jnp.broadcast_to(len_col, (32, 128))
    linv[...] = 1.0 / lens_s[...]

    pl.semaphore_wait(barrier, NF - 1 + NJ - 1)

    def at(x, y, c):
        return ((x + 4) % 4) * 8 + ((y + 4) % 4) * 2 + c

    def along(a, b):
        return at(jx + jnp.where(jc == 0, a, b), jy + jnp.where(jc == 0, b, a), jc)

    near = (0, 1, -1, 2)
    chip = {(a, b): along(a, b) for b in near for a in near}
    mate = at(jx, jy, 1 - jc)

    def block_copy(buf, ssem, rsem, slot, n, to):
        return remote(buf.at[slot], buf.at[slot], ssem.at[n], rsem.at[slot], to, f)

    @pl.loop(1, NF)
    def _(i):
        g = (f + i) % NF
        remote(wsl.at[g], wall.at[j, f], ws_sem.at[g], wr_sem.at[f], j, g).start()

    for n, c in enumerate(chip.values()):
        if n:
            block_copy(emball, es_sem, er_sem, j, n, c).start()
    block_copy(emball, es_sem, er_sem, j, 0, mate).start()
    own_w = pltpu.make_async_copy(wsl.at[f], wall.at[j, f], c_sem.at[0])
    own_q = pltpu.make_async_copy(q_ref, qz.at[f], c_sem.at[1])
    own_w.start()
    own_q.start()

    own_w.wait()

    @pl.loop(1, NF)
    def _(i):
        g = (f + i) % NF
        remote(wsl.at[g], wall.at[j, g], ws_sem.at[g], wr_sem.at[g], j, g).wait_recv()

    @pl.loop(1, NF)
    def _(i):
        g = (f + i) % NF
        remote(q_ref, qz.at[f], qs_sem.at[g], qr_sem.at[f], j, g).start()

    sent_w = []

    def send_w(slot, to):
        block_copy(wall, gs_sem, gr_sem, slot, len(sent_w), to).start()
        sent_w.append((slot, to))

    def wait_w(slot):
        block_copy(wall, gs_sem, gr_sem, slot, 0, mate).wait_recv()

    for a in near[1:]:
        send_w(j, chip[a, 0])
    for b in near[1:]:
        send_w(j, chip[0, b])
    send_w(j, mate)
    for n, c in enumerate(chip.values()):
        if n:
            block_copy(emball, es_sem, er_sem, c, 0, mate).wait_recv()
            block_copy(emball, es_sem, er_sem, c, 16 + n, mate).start()
    for a in near[1:]:
        wait_w(chip[a, 0])
        for b in near[1:]:
            send_w(chip[a, 0], chip[0, b])
        send_w(chip[a, 0], mate)
    r64, s64 = iota((64, 512), 0), iota((64, 512), 1)
    spread = jnp.where(iota((128, 512), 0) == HID - 256 + iota((128, 512), 1) // 16 * 2 + iota((128, 512), 1) % 2, 1.0, 0.0).astype(BF16)
    ids = [wall[j, g, :, 256:LANES].astype(F32) for g in range(NF)]
    id64 = jnp.concatenate([jnp.broadcast_to(v[0:1], (8, 128)) for v in ids], axis=0)
    qi64 = jnp.concatenate([jnp.broadcast_to(v[1:2], (8, 128)) for v in ids], axis=0)
    id_of = dot(id64.astype(BF16), spread)
    asker = (s64 // 2) % 8 == r64 // 8
    mine = (id_of >= 0.0) & (dot(qi64.astype(BF16), spread).astype(I32) == r64 % 4) & asker
    mine_s[...] = jnp.where(mine, 1.0, 0.0)
    id_row = jnp.sum(jnp.where(asker & (r64 % 8 == 0), id_of, 0.0), axis=0, keepdims=True)

    @pl.loop(0, 16)
    def _(n):
        block_copy(emball, es_sem, er_sem, n * 2 + 1 - jc, 0, mate).wait_recv()

    for g in range(4):
        hot = (iota((256, 128), 0) // 32 == iota((256, 128), 1) // 16)
        hot = hot & ((iota((256, 128), 0) % 32).astype(F32) == id_row[:, g * 128 : (g + 1) * 128])
        rows = emball[g * 8 : (g + 1) * 8].reshape(256, 256)
        hot = jnp.where(hot, 1.0, 0.0).astype(BF16)
        part = lax.dot_general(hot, rows, (((0,), (0,)), ((), ())), preferred_element_type=F32)
        ev_s[g * 128 : (g + 1) * 128, :] = part.astype(BF16)
    for a in near:
        for b in near[1:]:
            wait_w(chip[a, b])
            send_w(chip[a, b], mate)

    @pl.loop(0, 16)
    def _(n):
        wait_w(n * 2 + 1 - jc)

    @pl.loop(0, NJ)
    def _(k):
        for h in range(4):
            pair = jnp.concatenate([wall[k, 2 * h].astype(F32), wall[k, 2 * h + 1].astype(F32)], axis=0)
            w2[pl.ds(pl.multiple_of(k * 64 + h * 16, 16), 16), :] = pair.astype(BF16)
            for e in range(2):
                tab[pl.ds(k * 8 + 2 * h + e, 1), :] = pair[8 * e : 8 * e + 1, 256:LANES]
                tab[pl.ds(256 + k * 8 + 2 * h + e, 1), :] = pair[8 * e + 1 : 8 * e + 2, 256:LANES]

    own_q.wait()

    @pl.loop(1, NF)
    def _(i):
        g = (f + i) % NF
        remote(q_ref, qz.at[g], qs_sem.at[g], qr_sem.at[g], j, g).wait_recv()

    q4 = [qz[g].astype(F32) for g in range(NF)]
    q32 = jnp.concatenate(q4, axis=0).astype(BF16)
    q_own = dot(q32, w2[...]) * GELU_SCALE
    qw[j, 0:32, :] = q_own[:, 0:128]
    qw[j, 32:64, :] = q_own[:, 128:256]
    third = jnp.where(iota((16, 128), 1) < 64, q_own[0:16, 256:384], pltpu.roll(q_own[16:32, 256:384], 64, 1))
    qw[j, 64:80, :] = third

    pick = (iota((8, 128), 1) == HID - 256 + 2 * j + iota((8, 128), 0)) & (iota((8, 128), 0) < 2)
    asked = dot_nt(jnp.where(pick, 1.0, 0.0).astype(BF16), tab[...].astype(BF16))
    cidv[...] = asked.astype(I32)
    to_smem = pltpu.make_async_copy(cidv, cid, c_sem.at[2])
    to_smem.start()
    sent_q = []

    def send_q(slot, to):
        block_copy(qw, hs_sem, hr_sem, slot, len(sent_q), to).start()
        sent_q.append((slot, to))

    for a in near[1:]:
        send_q(j, chip[a, 0])
    for b in near[1:]:
        send_q(j, chip[0, b])
    send_q(j, mate)

    loads[6].wait()

    @pl.loop(0, 4)
    def _(p):
        rows = pl.ds(pl.multiple_of(p * 160, 16), 160)
        part = dot(x_s[rows, :], w2[...]) * GELU_SCALE
        for b in range(3):
            tw0[b, rows, :] = part[:, b * 128 : (b + 1) * 128]

    @pl.loop(0, 8)
    def _(p):
        for i in range(4):
            c = p * 4 + i
            length = lens_s[pl.ds(c, 1), :]
            valid = iota((24, 128), 0).astype(F32) < length
            for b in range(2):
                tw[c, :, b * 128 : (b + 1) * 128] = jnp.where(valid, tw0[b, pl.ds(c, 24, stride=32), :], FAR)
            row, low = iota((16, 128), 0), iota((16, 128), 1) < 64
            token = jnp.where(low, row, row + 10)
            valid = (row < 10) & (token.astype(F32) < length)
            early, late = tw0[2, pl.ds(c, 16, stride=32), :], tw0[2, pl.ds(c + 320, 16, stride=32), :]
            tw3[c] = jnp.where(valid, jnp.where(low, early, pltpu.roll(late, 64, 1)), FAR)

    for a in near[1:]:
        block_copy(qw, hs_sem, hr_sem, chip[a, 0], 0, mate).wait_recv()
        for b in near[1:]:
            send_q(chip[a, 0], chip[0, b])
        send_q(chip[a, 0], mate)
    to_smem.wait()

    q64 = jnp.concatenate([qz[g, :, pl.ds(pl.multiple_of(f * 256, 256), 256)].astype(F32) for g in range(NF) for _ in range(2)], axis=0)
    sc = dot_nt(q64.astype(BF16), ev_s[...])
    srow[...] = jnp.sum(jnp.where((mine_s[...] > 0.5) & ((r64 // 4) % 2 == 0), sc, 0.0), axis=0, keepdims=True)

    @pl.loop(1, NF)
    def _(i):
        g = (f + i) % NF
        remote(srow, sall.at[f], ss_sem.at[g], sr_sem.at[f], j, g).start()

    lane16 = iota((16, LANES), 1)
    ro16 = ros[f]
    ro_row = ro16[0:1]

    def send_block(k):
        remote(rsend.at[k], rall.at[j], rs_sem.at[k], rr_sem.at[j], k, f).start()

    def pair(y):
        y2 = y * y
        z = (y * BETA) * y2
        u = y + z
        t = jnp.tanh(u)
        c1 = 1.0 + t
        return c1 * ((1.0 - t) * (u + (z + z)) + 1.0), c1 * y

    acc[...] = jnp.zeros_like(acc)
    lvs[...] = jnp.zeros_like(lvs)

    def finish(half, k):
        inv = lvs[half]
        sums = []
        for b in range(4):
            part = [acc[half, b, pl.ds(r, 16, stride=8), :] for r in range(8)]
            part = [part[r] + part[r + 4] for r in range(4)]
            sums.append(((part[0] + part[2]) + (part[1] + part[3])) * inv)
        sums[2] = sums[2] + pltpu.roll(sums[2], 64, 1)
        like = jnp.sum(sums[3], axis=1, keepdims=True) * (0.5 / GELU_SCALE)
        summed = (jnp.concatenate(sums[0:3], axis=1) * 0.5) * ro_row
        hi = like.astype(BF16).astype(F32)
        mid = (like - hi).astype(BF16).astype(F32)
        low = like - hi - mid
        summed = jnp.where(lane16 >= HID, 0.0, summed)
        summed = jnp.where(lane16 == HID, hi, summed)
        summed = jnp.where(lane16 == HID + 1, mid, summed)
        summed = jnp.where(lane16 == HID + 2, low, summed)
        rsend[k] = summed.astype(BF16)

    def is_mate(i):
        return ((i % 2 == 0) & (i > 0)) | (i == NJ - 1)

    def block_at(i):
        p = jnp.where(is_mate(i), jnp.where(i == NJ - 1, 15, i // 2 - 1), (i + 1) // 2)
        t = p - 7
        m = jnp.where(p < 4, p, jnp.where(p < 7, 0, 1 + t % 3))
        n = jnp.where(p < 4, 0, jnp.where(p < 7, p - 3, 1 + t // 3))
        a, b = m + (m // 2) * (1 - 2 * (m % 2)), n + (n // 2) * (1 - 2 * (n % 2))
        c = jnp.where(is_mate(i), 1 - jc, jc)
        return at(jx + jnp.where(c == 0, a, b), jy + jnp.where(c == 0, b, a), c)

    def do_block(i, half):
        k = block_at(i)

        @pl.when(is_mate(i) | ((i + 1) // 2 > 3))
        def _():
            block_copy(qw, hs_sem, hr_sem, k, 0, mate).wait_recv()

        @pl.when((i > 0) & jnp.logical_not(is_mate(i)) & ((i + 1) // 2 > 3))
        def _():
            block_copy(qw, hs_sem, hr_sem, k, 24 + (i + 1) // 2, mate).start()

        qcur[:, 0:128] = qw[k, 0:32, :]
        qcur[:, 128:256] = qw[k, 32:64, :]
        third = qw[k, 64:80, :]
        swap = pltpu.roll(third, 64, 1)
        qcur[0:16, 256:384] = jnp.where(iota((16, 128), 1) < 64, third, swap)
        qcur[16:32, 256:384] = jnp.where(iota((16, 128), 1) < 64, swap, third)
        finish(1 - half, block_at((i + NJ - 1) % NJ))
        for s in range(16):
            d, e = s // 2, s % 2
            c = jnp.clip(cid[e, k * 8 + d], 0, 31)
            q = jnp.clip(cid[e, 256 + k * 8 + d], 0, 3)
            q_row = qcur[pl.ds(d * 4 + q, 1), :]
            slope, value = pair(tw[c] + q_row[:, 0:256])
            slope3, value3 = pair(tw3[c] + q_row[:, 256:384])
            slope = slope[0:8] + slope[8:16] + slope[16:24]
            value = (value[0:8] + value[8:16] + value[16:24]) * ro16[:, 0:256]
            value3 = (value3[0:8] + value3[8:16]) * ro16[:, 256:384]
            at8 = pl.ds(s * 8, 8)
            acc[half, 0, at8, :] = slope[:, 0:128]
            acc[half, 1, at8, :] = slope[:, 128:256]
            acc[half, 2, at8, :] = slope3[0:8] + slope3[8:16]
            acc[half, 3, at8, :] = value[:, 0:128] + value[:, 128:256] + value3
            lvs[half, pl.ds(s, 1), :] = linv[pl.ds(c, 1), :]

        @pl.when(i > 1)
        def _():
            send_block(block_at(i - 1))

    @pl.loop(0, NJ // 2)
    def _(n):
        do_block(2 * n, 0)
        do_block(2 * n + 1, 1)

    finish((NJ - 1) % 2, block_at(NJ - 1))
    own_r_copy = pltpu.make_async_copy(rsend.at[j], rall.at[j], c_sem.at[4])
    own_r_copy.start()
    send_block(block_at(NJ - 1))

    own_r_copy.wait()

    @pl.loop(1, NJ)
    def _(i):
        k = (j + i) % NJ
        remote(rsend.at[k], rall.at[k], rs_sem.at[k], rr_sem.at[k], k, f).wait_recv()

    rv = rall[...].reshape(NJ * 16, LANES)
    lp = (iota((8, LANES), 1) >= HID) & (iota((8, LANES), 1) < HID + 3)
    like_row = dot_nt(jnp.where(lp, 1.0, 0.0).astype(BF16), rv)[0:1]
    zrow[...] = like_row

    @pl.loop(1, NF)
    def _(i):
        g = (f + i) % NF
        remote(zrow, zall.at[f], ls_sem.at[g], lr_sem.at[f], j, g).start()

    zall[f] = zrow[...]
    sall[f] = srow[...]

    @pl.loop(1, NF)
    def _(i):
        g = (f + i) % NF
        remote(srow, sall.at[g], ss_sem.at[g], sr_sem.at[g], j, g).wait_recv()
        remote(zrow, zall.at[g], ls_sem.at[g], lr_sem.at[g], j, g).wait_recv()

    total, score = zall[0], sall[0]
    for g in range(1, NF):
        total, score = total + zall[g], score + sall[g]
    mine = mine_s[...] > 0.5
    retrieve = jnp.broadcast_to(score, (64, 512)) * (1.0 / math.sqrt(2048.0))
    joined = retrieve + jnp.broadcast_to(total, (64, 512))

    def softmax(v):
        top = jnp.max(jnp.where(mine, v, -3.0e38), axis=1, keepdims=True)
        ex = jnp.where(mine, jnp.exp(jnp.where(mine, v - top, 0.0)), 0.0)
        norm = jnp.sum(ex, axis=1, keepdims=True)
        return ex / norm, top + jnp.log(norm)

    prior, lse_r = softmax(retrieve)
    post, lse_j = softmax(joined)
    loss = lse_r - lse_j
    own_row = (iota((64, 128), 0) == f * 8 + iota((64, 128), 1)) & (iota((64, 128), 1) < 4)
    loss_ref[...] = jnp.sum(jnp.where(own_row, loss, 0.0), axis=0, keepdims=True)[:, 0:4]

    hi, lo = two(post)
    mix = dot(hi, rv) + dot(lo, rv)
    mix = jnp.where(iota((64, LANES), 1) < HID, mix, 0.0)
    hi, lo = two(mix)
    fhi, flo = two((prior - post) * (LOSS_SCALE / math.sqrt(2048.0)))
    first = dot(fhi, ev_s[...]) + dot(flo, ev_s[...])
    upper = (iota((64, 256), 0) // 4) % 2 == 1
    for b in range(4):
        w_lo, w_hi = w2[b * 256 : (b + 1) * 256, :], w2[1024 + b * 256 : 1024 + (b + 1) * 256, :]
        part = jnp.where(upper, dot_nt(hi, w_hi) + dot_nt(lo, w_hi), dot_nt(hi, w_lo) + dot_nt(lo, w_lo))
        place = ((f % 4) == b) & (upper == (f // 4 == 1))
        part = jnp.where(place, first, 0.0) - LOSS_SCALE * part
        outp[b] = part.reshape(NF, 8, 256)

        @pl.loop(1, NF)
        def _(i):
            g = (f + i) % NF
            remote(outp.at[b, g], orec.at[b, f], os_sem.at[b, g], or_sem.at[b, f], j, g).start()

    for n, (slot, to) in enumerate(sent_w):
        block_copy(wall, gs_sem, gr_sem, slot, n, to).wait_send()

    for n, (slot, to) in enumerate(sent_q):
        block_copy(qw, hs_sem, hr_sem, slot, n, to).wait_send()

    @pl.loop(4, 16)
    def _(n):
        block_copy(qw, hs_sem, hr_sem, j, 24 + n, mate).wait_send()

    @pl.loop(0, 32)
    def _(n):
        @pl.when(n != 16)
        def _():
            block_copy(emball, es_sem, er_sem, j, n, mate).wait_send()

    @pl.loop(1, NJ)
    def _(i):
        k = (j + i) % NJ
        remote(rsend.at[k], rall.at[k], rs_sem.at[k], rr_sem.at[k], k, f).wait_send()

    @pl.loop(1, NF)
    def _(i):
        g = (f + i) % NF
        remote(wsl.at[g], wall.at[j, g], ws_sem.at[g], wr_sem.at[g], j, g).wait_send()
        remote(q_ref, qz.at[g], qs_sem.at[g], qr_sem.at[g], j, g).wait_send()
        remote(zrow, zall.at[g], ls_sem.at[g], lr_sem.at[g], j, g).wait_send()
        remote(srow, sall.at[g], ss_sem.at[g], sr_sem.at[g], j, g).wait_send()

    for b in range(4):

        @pl.loop(1, NF)
        def _(i):
            g = (f + i) % NF
            remote(outp.at[b, g], orec.at[b, g], os_sem.at[b, g], or_sem.at[b, g], j, g).wait()

        orec[b, f] = outp[b, f]
        whole = orec[b, 0]
        for g in range(1, NF):
            whole = whole + orec[b, g]
        grad_ref[:, b * 256 : (b + 1) * 256] = whole[0:4]
        grad_ref[:, 1024 + b * 256 : 1024 + (b + 1) * 256] = whole[4:8]


def on_device(queries, candidates, tables, lengths, passage_embed, reader_weight, readout):
    vm = pl.BlockSpec(memory_space=pltpu.VMEM)
    dma = pltpu.SemaphoreType.DMA
    grad, loss = pl.pallas_call(
        kernel,
        out_shape=(jax.ShapeDtypeStruct((4, 2048), F32), jax.ShapeDtypeStruct((1, 4), F32)),
        in_specs=[pl.BlockSpec(memory_space=pltpu.HBM)] * 7,
        out_specs=(vm, vm),
        scratch_shapes=[
            pltpu.VMEM((8, 2560), BF16),
            pltpu.VMEM((4, 2048), BF16),
            pltpu.VMEM((4, 8), I32),
            pltpu.VMEM((1, 32), I32),
            pltpu.VMEM((20, 128), F32),
            pltpu.VMEM((NF, 8, LANES), BF16),
            pltpu.VMEM((NF, 8, LANES), F32),
            pltpu.VMEM((NF, 4, 2048), BF16),
            pltpu.VMEM((NJ, NF, 8, LANES), BF16),
            pltpu.VMEM((2048, LANES), BF16),
            pltpu.VMEM((640, 2048), BF16),
            pltpu.VMEM((3, 832, 128), F32),
            pltpu.VMEM((32, 24, 256), F32),
            pltpu.VMEM((32, 16, 128), F32),
            pltpu.VMEM((NJ, 80, 128), F32),
            pltpu.VMEM((32, 128), F32),
            pltpu.VMEM((8, 512), I32),
            pltpu.SMEM((8, 512), I32),
            pltpu.VMEM((32, 128), F32),
            pltpu.VMEM((NJ, 32, 256), BF16),
            pltpu.VMEM((512, 256), BF16),
            pltpu.VMEM((64, 512), F32),
            pltpu.VMEM((2, 4, 128, 128), F32),
            pltpu.VMEM((2, 16, 128), F32),
            pltpu.VMEM((NJ, 16, LANES), BF16),
            pltpu.VMEM((NJ, 16, LANES), BF16),
            pltpu.VMEM((1, 512), F32),
            pltpu.VMEM((NF, 1, 512), F32),
            pltpu.VMEM((1, 512), F32),
            pltpu.VMEM((NF, 1, 512), F32),
            pltpu.VMEM((4, NF, 8, 256), F32),
            pltpu.VMEM((4, NF, 8, 256), F32),
            pltpu.VMEM((512, 128), F32),
            pltpu.VMEM((32, LANES), F32),
            dma((NF,)), dma((NF,)), dma((NF,)), dma((NF,)),
            dma((48,)), dma((NJ,)), dma((40,)), dma((NJ,)),
            dma((NJ,)), dma((NJ,)), dma((NJ,)), dma((NJ,)),
            dma((NF,)), dma((NF,)), dma((4, NF)), dma((4, NF)), dma((5,)), dma((7,)), dma((NF,)), dma((NF,)),
        ],
        compiler_params=pltpu.CompilerParams(collective_id=0, has_side_effects=True, vmem_limit_bytes=67043328),
    )(
        reader_weight,
        queries,
        candidates,
        tables.transpose(1, 0, 2).reshape(640, 2048),
        lengths.reshape(1, 32),
        passage_embed,
        readout.reshape(20, 128),
    )
    return grad, loss.reshape(4)


def solution(mesh):
    both = ("corpus", "fsdp")
    in_specs = (P(both, None), P(both, None), P("corpus", None, None), P("corpus"), P("corpus", None), P(both, None), P())
    return jax.shard_map(
        on_device, mesh=mesh, in_specs=in_specs, out_specs=(P(both, None), P(both)), check_vma=False
    )
```

```python
import functools
import math

import jax
import jax.numpy as jnp
from jax import lax
from jax.experimental import pallas as pl
from jax.experimental.pallas import tpu as pltpu
from jax.sharding import PartitionSpec as P

GELU_SCALE = math.sqrt(2.0 / math.pi)
GELU_CUBIC = 0.044715
LOSS_SCALE = 64.0
BETA = GELU_CUBIC / (GELU_SCALE * GELU_SCALE)
FAR = -1.0e5

MESH = pl.DeviceIdType.MESH
F32 = jnp.float32
BF16 = jnp.bfloat16
I32 = jnp.int32
NJ, NF = 32, 8
HID = 320
LANES = 384
SLOTS = NJ * 2


def iota(shape, dim):
    return lax.broadcasted_iota(I32, shape, dim)


def dot_nt(a, b):
    return lax.dot_general(a, b, (((1,), (1,)), ((), ())), preferred_element_type=F32)


def dot(a, b):
    return jnp.dot(a, b, preferred_element_type=F32)


def two(x):
    hi = x.astype(BF16)
    return hi, (x - hi.astype(F32)).astype(BF16)


def kernel(
    w_hbm, q_hbm, cand_hbm, tab_hbm, len_hbm, emb_hbm, ro_hbm,
    grad_ref, loss_ref,
    w_ref, q_ref, cand_ref, len_ref, ro_ref, wsl, ros, qz, wall, w2, x_s, tw0, tw, tw3, qw, linv, cidv, cid, lens_s, emball, ev_s, mine_s, acc, lvs, rsend, rall,
    zrow, zall, srow, sall, outp, orec, tab, qcur, q32,
    ws_sem, wr_sem, qs_sem, qr_sem, gs_sem, gr_sem, hs_sem, hr_sem, es_sem, er_sem, rs_sem, rr_sem,
    ls_sem, lr_sem, os_sem, or_sem, c_sem, i_sem, ss_sem, sr_sem,
):
    j = lax.axis_index("corpus")
    f = lax.axis_index("fsdp")
    jx, jy, jc = j // 8, (j // 2) % 4, j % 2

    def remote(src, dst, ssem, rsem, jj, ff):
        return pltpu.make_async_remote_copy(
            src_ref=src, dst_ref=dst, send_sem=ssem, recv_sem=rsem, device_id=(jj, ff), device_id_type=MESH
        )

    pairs = ((cand_hbm, cand_ref), (w_hbm, w_ref), (ro_hbm, ro_ref), (len_hbm, len_ref), (q_hbm, q_ref))
    pairs = pairs + ((emb_hbm.at[:, pl.ds(pl.multiple_of(f * 256, 256), 256)], emball.at[j]), (tab_hbm, x_s))
    loads = [pltpu.make_async_copy(a, b, i_sem.at[n]) for n, (a, b) in enumerate(pairs)]
    for load in loads:
        load.start()
    barrier = pltpu.get_barrier_semaphore()

    @pl.loop(1, NF)
    def _(i):
        pl.semaphore_signal(barrier, inc=1, device_id=(j, (f + i) % NF), device_id_type=MESH)

    @pl.loop(1, NJ)
    def _(i):
        pl.semaphore_signal(barrier, inc=1, device_id=((j + i) % NJ, f), device_id_type=MESH)

    for load in loads[:6]:
        load.wait()

    cand = cand_ref[...].astype(F32)
    wide = jnp.concatenate([jnp.broadcast_to(cand[i : i + 1], (8, 8)) for i in range(4)], axis=0)
    eye = iota((32, 32), 0) == iota((32, 32), 1)
    idc = jnp.sum(jnp.where(iota((32, 8), 0) % 8 == iota((32, 8), 1), wide, 0.0), axis=1, keepdims=True)
    idr = jnp.sum(jnp.where(eye, idc, 0.0), axis=0, keepdims=True).astype(I32)
    idc = idc.astype(I32)
    own_r, own_c = idr // 32, idc // 32
    same = (own_c == own_r) & (iota((32, 32), 1) < iota((32, 32), 0))
    earlier = jnp.sum(jnp.where(same, 1, 0).astype(F32), axis=1, keepdims=True).astype(I32)
    lane_of = own_c * 2 + earlier + HID
    at_slot = lane_of == iota((32, LANES), 1)
    id_lane = jnp.sum(jnp.where(at_slot, (idc % 32 + 1).astype(F32), 0.0), axis=0, keepdims=True) - 1.0
    q_lane = jnp.sum(jnp.where(at_slot, (iota((32, LANES), 0) // 8).astype(F32), 0.0), axis=0, keepdims=True)
    row8, lane8 = iota((8, LANES), 0), iota((8, LANES), 1)
    tail = jnp.where(row8 == 0, id_lane, jnp.where(row8 == 1, q_lane, 0.0))
    w_own = w_ref[...].astype(F32)
    for g in range(NF):
        base, off = g * HID // 128 * 128, g * HID % 128
        seg, b = w_own[:, base : base + LANES], base // 128
        rseg = jnp.concatenate([jnp.broadcast_to(ro_ref[b + i : b + i + 1], (8, 128)) for i in range(3)], axis=1)
        if off:
            seg, rseg = pltpu.roll(seg, LANES - off, 1), pltpu.roll(rseg, LANES - off, 1)
        wsl[g] = jnp.where(lane8 < HID, seg, tail).astype(BF16)
        ros[g] = jnp.where(lane8 < HID, rseg, pltpu.roll(rseg, 64, 1))
    len_col = jnp.sum(jnp.where(eye, len_ref[...].astype(F32), 0.0), axis=1, keepdims=True)
    lens_s[...] = jnp.broadcast_to(len_col, (32, 128))
    linv[...] = 1.0 / lens_s[...]

    pl.semaphore_wait(barrier, NF - 1 + NJ - 1)

    def at(x, y, c):
        return ((x + 4) % 4) * 8 + ((y + 4) % 4) * 2 + c

    def along(a, b):
        return at(jx + jnp.where(jc == 0, a, b), jy + jnp.where(jc == 0, b, a), jc)

    near = (0, 1, -1, 2)
    chip = {(a, b): along(a, b) for b in near for a in near}
    mate = at(jx, jy, 1 - jc)

    def block_copy(buf, ssem, rsem, slot, n, to):
        return remote(buf.at[slot], buf.at[slot], ssem.at[n], rsem.at[slot], to, f)

    @pl.loop(1, NF)
    def _(i):
        g = (f + i) % NF
        remote(wsl.at[g], wall.at[j, f], ws_sem.at[g], wr_sem.at[f], j, g).start()

    for n, c in enumerate(chip.values()):
        if n:
            block_copy(emball, es_sem, er_sem, j, n, c).start()
    block_copy(emball, es_sem, er_sem, j, 0, mate).start()
    own_w = pltpu.make_async_copy(wsl.at[f], wall.at[j, f], c_sem.at[0])
    own_q = pltpu.make_async_copy(q_ref, qz.at[f], c_sem.at[1])
    own_w.start()
    own_q.start()

    own_w.wait()

    @pl.loop(1, NF)
    def _(i):
        g = (f + i) % NF
        remote(wsl.at[g], wall.at[j, g], ws_sem.at[g], wr_sem.at[g], j, g).wait_recv()

    @pl.loop(1, NF)
    def _(i):
        g = (f + i) % NF
        remote(q_ref, qz.at[f], qs_sem.at[g], qr_sem.at[f], j, g).start()

    sent_w = []

    def send_w(slot, to):
        block_copy(wall, gs_sem, gr_sem, slot, len(sent_w), to).start()
        sent_w.append((slot, to))

    def wait_w(slot):
        block_copy(wall, gs_sem, gr_sem, slot, 0, mate).wait_recv()

    def unpack(k):
        for h in range(4):
            pair = jnp.concatenate([wall[k, 2 * h].astype(F32), wall[k, 2 * h + 1].astype(F32)], axis=0)
            w2[pl.ds(pl.multiple_of(k * 64 + h * 16, 16), 16), :] = pair.astype(BF16)
            for e in range(2):
                tab[pl.ds(k * 8 + 2 * h + e, 1), :] = pair[8 * e : 8 * e + 1, 256:LANES]
                tab[pl.ds(256 + k * 8 + 2 * h + e, 1), :] = pair[8 * e + 1 : 8 * e + 2, 256:LANES]

    for a in near[1:]:
        send_w(j, chip[a, 0])
    for b in near[1:]:
        send_w(j, chip[0, b])
    send_w(j, mate)
    for n, c in enumerate(chip.values()):
        if n:
            block_copy(emball, es_sem, er_sem, c, 0, mate).wait_recv()
            block_copy(emball, es_sem, er_sem, c, 16 + n, mate).start()
    for a in near[1:]:
        wait_w(chip[a, 0])
        for b in near[1:]:
            send_w(chip[a, 0], chip[0, b])
        send_w(chip[a, 0], mate)
    unpack(j)
    for a in near[1:]:
        unpack(chip[a, 0])

    r64, s64 = iota((64, 512), 0), iota((64, 512), 1)
    spread = jnp.where(iota((128, 512), 0) == HID - 256 + iota((128, 512), 1) // 16 * 2 + iota((128, 512), 1) % 2, 1.0, 0.0).astype(BF16)
    ids = [wall[j, g, :, 256:LANES].astype(F32) for g in range(NF)]
    id64 = jnp.concatenate([jnp.broadcast_to(v[0:1], (8, 128)) for v in ids], axis=0)
    qi64 = jnp.concatenate([jnp.broadcast_to(v[1:2], (8, 128)) for v in ids], axis=0)
    id_of = dot(id64.astype(BF16), spread)
    asker = (s64 // 2) % 8 == r64 // 8
    mine = (id_of >= 0.0) & (dot(qi64.astype(BF16), spread).astype(I32) == r64 % 4) & asker
    mine_s[...] = jnp.where(mine, 1.0, 0.0)
    id_row = jnp.sum(jnp.where(asker & (r64 % 8 == 0), id_of, 0.0), axis=0, keepdims=True)

    @pl.loop(0, 16)
    def _(n):
        block_copy(emball, es_sem, er_sem, n * 2 + 1 - jc, 0, mate).wait_recv()

    for g in range(4):
        hot = (iota((256, 128), 0) // 32 == iota((256, 128), 1) // 16)
        hot = hot & ((iota((256, 128), 0) % 32).astype(F32) == id_row[:, g * 128 : (g + 1) * 128])
        rows = emball[g * 8 : (g + 1) * 8].reshape(256, 256)
        hot = jnp.where(hot, 1.0, 0.0).astype(BF16)
        part = lax.dot_general(hot, rows, (((0,), (0,)), ((), ())), preferred_element_type=F32)
        ev_s[g * 128 : (g + 1) * 128, :] = part.astype(BF16)
    for a in near:
        for b in near[1:]:
            wait_w(chip[a, b])
            send_w(chip[a, b], mate)
            unpack(chip[a, b])

    own_q.wait()

    @pl.loop(1, NF)
    def _(i):
        g = (f + i) % NF
        remote(q_ref, qz.at[g], qs_sem.at[g], qr_sem.at[g], j, g).wait_recv()

    q4 = [qz[g].astype(F32) for g in range(NF)]
    q32[...] = jnp.concatenate(q4, axis=0).astype(BF16)
    q64 = jnp.concatenate([qz[g, :, pl.ds(pl.multiple_of(f * 256, 256), 256)].astype(F32) for g in range(NF) for _ in range(2)], axis=0)
    sc = dot_nt(q64.astype(BF16), ev_s[...])
    srow[...] = jnp.sum(jnp.where((mine_s[...] > 0.5) & ((r64 // 4) % 2 == 0), sc, 0.0), axis=0, keepdims=True)

    @pl.loop(1, NF)
    def _(i):
        g = (f + i) % NF
        remote(srow, sall.at[f], ss_sem.at[g], sr_sem.at[f], j, g).start()

    @pl.loop(0, 16)
    def _(n):
        wait_w(n * 2 + 1 - jc)
        unpack(n * 2 + 1 - jc)

    q_own = dot(q32[...], w2[...]) * GELU_SCALE
    qw[j, 0:32, :] = q_own[:, 0:128]
    qw[j, 32:64, :] = q_own[:, 128:256]
    third = jnp.where(iota((16, 128), 1) < 64, q_own[0:16, 256:384], pltpu.roll(q_own[16:32, 256:384], 64, 1))
    qw[j, 64:80, :] = third

    pick = (iota((8, 128), 1) == HID - 256 + 2 * j + iota((8, 128), 0)) & (iota((8, 128), 0) < 2)
    asked = dot_nt(jnp.where(pick, 1.0, 0.0).astype(BF16), tab[...].astype(BF16))
    cidv[...] = asked.astype(I32)
    to_smem = pltpu.make_async_copy(cidv, cid, c_sem.at[2])
    to_smem.start()
    sent_q = []

    def send_q(slot, to):
        block_copy(qw, hs_sem, hr_sem, slot, len(sent_q), to).start()
        sent_q.append((slot, to))

    for a in near[1:]:
        send_q(j, chip[a, 0])
    for b in near[1:]:
        send_q(j, chip[0, b])
    send_q(j, mate)

    loads[6].wait()

    @pl.loop(0, 4)
    def _(p):
        rows = pl.ds(pl.multiple_of(p * 160, 16), 160)
        part = dot(x_s[rows, :], w2[...]) * GELU_SCALE
        for b in range(3):
            tw0[b, rows, :] = part[:, b * 128 : (b + 1) * 128]

    @pl.loop(0, 8)
    def _(p):
        for i in range(4):
            c = p * 4 + i
            length = lens_s[pl.ds(c, 1), :]
            valid = iota((24, 128), 0).astype(F32) < length
            for b in range(2):
                tw[c, :, b * 128 : (b + 1) * 128] = jnp.where(valid, tw0[b, pl.ds(c, 24, stride=32), :], FAR)
            row, low = iota((16, 128), 0), iota((16, 128), 1) < 64
            token = jnp.where(low, row, row + 10)
            valid = (row < 10) & (token.astype(F32) < length)
            early, late = tw0[2, pl.ds(c, 16, stride=32), :], tw0[2, pl.ds(c + 320, 16, stride=32), :]
            tw3[c] = jnp.where(valid, jnp.where(low, early, pltpu.roll(late, 64, 1)), FAR)

    for a in near[1:]:
        block_copy(qw, hs_sem, hr_sem, chip[a, 0], 0, mate).wait_recv()
        for b in near[1:]:
            send_q(chip[a, 0], chip[0, b])
        send_q(chip[a, 0], mate)
    to_smem.wait()

    lane16 = iota((16, LANES), 1)
    ro16 = ros[f]
    ro_row = ro16[0:1]

    def send_block(k):
        remote(rsend.at[k], rall.at[j], rs_sem.at[k], rr_sem.at[j], k, f).start()

    def pair(y):
        y2 = y * y
        z = (y * BETA) * y2
        u = y + z
        t = jnp.tanh(u)
        c1 = 1.0 + t
        return c1 * ((1.0 - t) * (u + (z + z)) + 1.0), c1 * y

    acc[...] = jnp.zeros_like(acc)
    lvs[...] = jnp.zeros_like(lvs)

    def finish(half, k):
        inv = lvs[half]
        sums = []
        for b in range(4):
            part = [acc[half, b, pl.ds(r, 16, stride=8), :] for r in range(8)]
            part = [part[r] + part[r + 4] for r in range(4)]
            sums.append(((part[0] + part[2]) + (part[1] + part[3])) * inv)
        sums[2] = sums[2] + pltpu.roll(sums[2], 64, 1)
        like = jnp.sum(sums[3], axis=1, keepdims=True) * (0.5 / GELU_SCALE)
        summed = (jnp.concatenate(sums[0:3], axis=1) * 0.5) * ro_row
        hi = like.astype(BF16).astype(F32)
        mid = (like - hi).astype(BF16).astype(F32)
        low = like - hi - mid
        summed = jnp.where(lane16 >= HID, 0.0, summed)
        summed = jnp.where(lane16 == HID, hi, summed)
        summed = jnp.where(lane16 == HID + 1, mid, summed)
        summed = jnp.where(lane16 == HID + 2, low, summed)
        rsend[k] = summed.astype(BF16)

    def ranked(r, c):
        t = jnp.maximum(r - 7, 0)
        m = jnp.where(r < 4, r, jnp.where(r < 7, 0, 1 + lax.rem(t, 3)))
        n = jnp.where(r < 4, 0, jnp.where(r < 7, r - 3, 1 + lax.div(t, 3)))
        m, n = jnp.where(m == 2, 3, jnp.where(m == 3, 2, m)), jnp.where(n == 2, 3, jnp.where(n == 3, 2, n))
        x, y = jnp.where(c == 0, m, n), jnp.where(c == 0, n, m)
        return lax.rem(jx + x, 4) * 8 + lax.rem(jy + y, 4) * 2 + c

    def do_block(k, last, half, started):
        qcur[:, 0:128] = qw[k, 0:32, :]
        qcur[:, 128:256] = qw[k, 32:64, :]
        third = qw[k, 64:80, :]
        swap = pltpu.roll(third, 64, 1)
        qcur[0:16, 256:384] = jnp.where(iota((16, 128), 1) < 64, third, swap)
        qcur[16:32, 256:384] = jnp.where(iota((16, 128), 1) < 64, swap, third)
        finish(1 - half, last)
        for s in range(16):
            d, e = s // 2, s % 2
            c = jnp.clip(cid[e, k * 8 + d], 0, 31)
            q = jnp.clip(cid[e, 256 + k * 8 + d], 0, 3)
            q_row = qcur[pl.ds(d * 4 + q, 1), :]
            slope, value = pair(tw[c] + q_row[:, 0:256])
            slope3, value3 = pair(tw3[c] + q_row[:, 256:384])
            slope = slope[0:8] + slope[8:16] + slope[16:24]
            value = (value[0:8] + value[8:16] + value[16:24]) * ro16[:, 0:256]
            value3 = (value3[0:8] + value3[8:16]) * ro16[:, 256:384]
            at8 = pl.ds(s * 8, 8)
            acc[half, 0, at8, :] = slope[:, 0:128]
            acc[half, 1, at8, :] = slope[:, 128:256]
            acc[half, 2, at8, :] = slope3[0:8] + slope3[8:16]
            acc[half, 3, at8, :] = value[:, 0:128] + value[:, 128:256] + value3
            lvs[half, pl.ds(s, 1), :] = linv[pl.ds(c, 1), :]

        @pl.when(started)
        def _():
            send_block(last)

    def two_blocks(r, carry):
        mine_k, last = carry
        later = ranked(jnp.minimum(r + 1, 15), jc)

        @pl.when((r > 2) & (r < 15))
        def _():
            block_copy(qw, hs_sem, hr_sem, later, 0, mate).wait_recv()
            block_copy(qw, hs_sem, hr_sem, later, 24 + r, mate).start()

        do_block(mine_k, last, 0, r > 0)
        other_k = ranked(r, 1 - jc)
        block_copy(qw, hs_sem, hr_sem, other_k, 0, mate).wait_recv()
        do_block(other_k, mine_k, 1, r > 0)
        return later, other_k

    final_k = ranked(15, 1 - jc)
    lax.fori_loop(0, 16, two_blocks, (j, final_k))
    finish(1, final_k)
    own_r_copy = pltpu.make_async_copy(rsend.at[j], rall.at[j], c_sem.at[4])
    own_r_copy.start()
    send_block(final_k)

    own_r_copy.wait()

    @pl.loop(1, NJ)
    def _(i):
        k = (j + i) % NJ
        remote(rsend.at[k], rall.at[k], rs_sem.at[k], rr_sem.at[k], k, f).wait_recv()

    rv = rall[...].reshape(NJ * 16, LANES)
    lp = (iota((8, LANES), 1) >= HID) & (iota((8, LANES), 1) < HID + 3)
    like_row = dot_nt(jnp.where(lp, 1.0, 0.0).astype(BF16), rv)[0:1]
    zrow[...] = like_row

    @pl.loop(1, NF)
    def _(i):
        g = (f + i) % NF
        remote(zrow, zall.at[f], ls_sem.at[g], lr_sem.at[f], j, g).start()

    zall[f] = zrow[...]
    sall[f] = srow[...]

    @pl.loop(1, NF)
    def _(i):
        g = (f + i) % NF
        remote(srow, sall.at[g], ss_sem.at[g], sr_sem.at[g], j, g).wait_recv()
        remote(zrow, zall.at[g], ls_sem.at[g], lr_sem.at[g], j, g).wait_recv()

    total, score = zall[0], sall[0]
    for g in range(1, NF):
        total, score = total + zall[g], score + sall[g]
    mine = mine_s[...] > 0.5
    retrieve = jnp.broadcast_to(score, (64, 512)) * (1.0 / math.sqrt(2048.0))
    joined = retrieve + jnp.broadcast_to(total, (64, 512))

    def softmax(v):
        top = jnp.max(jnp.where(mine, v, -3.0e38), axis=1, keepdims=True)
        ex = jnp.where(mine, jnp.exp(jnp.where(mine, v - top, 0.0)), 0.0)
        norm = jnp.sum(ex, axis=1, keepdims=True)
        return ex / norm, top + jnp.log(norm)

    prior, lse_r = softmax(retrieve)
    post, lse_j = softmax(joined)
    loss = lse_r - lse_j
    own_row = (iota((64, 128), 0) == f * 8 + iota((64, 128), 1)) & (iota((64, 128), 1) < 4)
    loss_ref[...] = jnp.sum(jnp.where(own_row, loss, 0.0), axis=0, keepdims=True)[:, 0:4]

    mix = dot(jnp.concatenate(two(post), axis=0), rv)
    mix = mix[0:64] + mix[64:128]
    mix = jnp.where(iota((64, LANES), 1) < HID, mix, 0.0)
    mix = jnp.concatenate(two(mix), axis=0)
    first = dot(jnp.concatenate(two((prior - post) * (LOSS_SCALE / math.sqrt(2048.0))), axis=0), ev_s[...])
    first = first[0:64] + first[64:128]
    upper = (iota((64, 256), 0) // 4) % 2 == 1
    for b in range(4):
        w_lo, w_hi = w2[b * 256 : (b + 1) * 256, :], w2[1024 + b * 256 : 1024 + (b + 1) * 256, :]
        up, down = dot_nt(mix, w_hi), dot_nt(mix, w_lo)
        part = jnp.where(upper, up[0:64] + up[64:128], down[0:64] + down[64:128])
        place = ((f % 4) == b) & (upper == (f // 4 == 1))
        part = jnp.where(place, first, 0.0) - LOSS_SCALE * part
        outp[b] = part.reshape(NF, 8, 256)

        @pl.loop(1, NF)
        def _(i):
            g = (f + i) % NF
            remote(outp.at[b, g], orec.at[b, f], os_sem.at[b, g], or_sem.at[b, f], j, g).start()

    for n, (slot, to) in enumerate(sent_w):
        block_copy(wall, gs_sem, gr_sem, slot, n, to).wait_send()

    for n, (slot, to) in enumerate(sent_q):
        block_copy(qw, hs_sem, hr_sem, slot, n, to).wait_send()

    @pl.loop(3, 15)
    def _(n):
        block_copy(qw, hs_sem, hr_sem, j, 24 + n, mate).wait_send()

    @pl.loop(0, 32)
    def _(n):
        @pl.when(n != 16)
        def _():
            block_copy(emball, es_sem, er_sem, j, n, mate).wait_send()

    @pl.loop(1, NJ)
    def _(i):
        k = (j + i) % NJ
        remote(rsend.at[k], rall.at[k], rs_sem.at[k], rr_sem.at[k], k, f).wait_send()

    @pl.loop(1, NF)
    def _(i):
        g = (f + i) % NF
        remote(wsl.at[g], wall.at[j, g], ws_sem.at[g], wr_sem.at[g], j, g).wait_send()
        remote(q_ref, qz.at[g], qs_sem.at[g], qr_sem.at[g], j, g).wait_send()
        remote(zrow, zall.at[g], ls_sem.at[g], lr_sem.at[g], j, g).wait_send()
        remote(srow, sall.at[g], ss_sem.at[g], sr_sem.at[g], j, g).wait_send()

    for b in range(4):

        @pl.loop(1, NF)
        def _(i):
            g = (f + i) % NF
            remote(outp.at[b, g], orec.at[b, g], os_sem.at[b, g], or_sem.at[b, g], j, g).wait()

        orec[b, f] = outp[b, f]
        whole = orec[b, 0]
        for g in range(1, NF):
            whole = whole + orec[b, g]
        grad_ref[:, b * 256 : (b + 1) * 256] = whole[0:4]
        grad_ref[:, 1024 + b * 256 : 1024 + (b + 1) * 256] = whole[4:8]


def on_device(queries, candidates, tables, lengths, passage_embed, reader_weight, readout):
    vm = pl.BlockSpec(memory_space=pltpu.VMEM)
    dma = pltpu.SemaphoreType.DMA
    grad, loss = pl.pallas_call(
        kernel,
        out_shape=(jax.ShapeDtypeStruct((4, 2048), F32), jax.ShapeDtypeStruct((1, 4), F32)),
        in_specs=[pl.BlockSpec(memory_space=pltpu.HBM)] * 7,
        out_specs=(vm, vm),
        scratch_shapes=[
            pltpu.VMEM((8, 2560), BF16),
            pltpu.VMEM((4, 2048), BF16),
            pltpu.VMEM((4, 8), I32),
            pltpu.VMEM((1, 32), I32),
            pltpu.VMEM((20, 128), F32),
            pltpu.VMEM((NF, 8, LANES), BF16),
            pltpu.VMEM((NF, 8, LANES), F32),
            pltpu.VMEM((NF, 4, 2048), BF16),
            pltpu.VMEM((NJ, NF, 8, LANES), BF16),
            pltpu.VMEM((2048, LANES), BF16),
            pltpu.VMEM((640, 2048), BF16),
            pltpu.VMEM((3, 832, 128), F32),
            pltpu.VMEM((32, 24, 256), F32),
            pltpu.VMEM((32, 16, 128), F32),
            pltpu.VMEM((NJ, 80, 128), F32),
            pltpu.VMEM((32, 128), F32),
            pltpu.VMEM((8, 512), I32),
            pltpu.SMEM((8, 512), I32),
            pltpu.VMEM((32, 128), F32),
            pltpu.VMEM((NJ, 32, 256), BF16),
            pltpu.VMEM((512, 256), BF16),
            pltpu.VMEM((64, 512), F32),
            pltpu.VMEM((2, 4, 128, 128), F32),
            pltpu.VMEM((2, 16, 128), F32),
            pltpu.VMEM((NJ, 16, LANES), BF16),
            pltpu.VMEM((NJ, 16, LANES), BF16),
            pltpu.VMEM((1, 512), F32),
            pltpu.VMEM((NF, 1, 512), F32),
            pltpu.VMEM((1, 512), F32),
            pltpu.VMEM((NF, 1, 512), F32),
            pltpu.VMEM((4, NF, 8, 256), F32),
            pltpu.VMEM((4, NF, 8, 256), F32),
            pltpu.VMEM((512, 128), F32),
            pltpu.VMEM((32, LANES), F32),
            pltpu.VMEM((32, 2048), BF16),
            dma((NF,)), dma((NF,)), dma((NF,)), dma((NF,)),
            dma((48,)), dma((NJ,)), dma((40,)), dma((NJ,)),
            dma((NJ,)), dma((NJ,)), dma((NJ,)), dma((NJ,)),
            dma((NF,)), dma((NF,)), dma((4, NF)), dma((4, NF)), dma((5,)), dma((7,)), dma((NF,)), dma((NF,)),
        ],
        compiler_params=pltpu.CompilerParams(collective_id=0, has_side_effects=True, vmem_limit_bytes=40 << 20),
    )(
        *[
            pltpu.with_memory_space_constraint(v, pltpu.HBM)
            for v in (
                reader_weight,
                queries,
                candidates,
                tables.transpose(1, 0, 2).reshape(640, 2048),
                lengths.reshape(1, 32),
                passage_embed,
                readout.reshape(20, 128),
            )
        ]
    )
    return grad, loss.reshape(4)


def solution(mesh):
    both = ("corpus", "fsdp")
    in_specs = (P(both, None), P(both, None), P("corpus", None, None), P("corpus"), P("corpus", None), P(both, None), P())
    return jax.shard_map(
        on_device, mesh=mesh, in_specs=in_specs, out_specs=(P(both, None), P(both)), check_vma=False
    )
```
